32 devices in a mesh: groups: 2 (over x), pos: 16 (over z, y, core).
Axes of the slice: x: 2, y: 2, z: 4, core: 2. Of those that a mesh axis runs over, the one named last changes fastest.
Arguments:
- activations: bfloat16 [32768, 512], P(('groups', 'pos')), parts along dimension 0, may hold values from -6 to 6
- kernel: bfloat16 [512, 5, 608], P('pos'), may hold values from -0.125 to 0.125
- cotangent: bfloat16 [16384, 608], P(('groups', 'pos')), parts along dimension 0, may hold values from -6 to 6
Outputs:
- pooled: bfloat16 [16384, 608], P(('groups', 'pos')), parts along dimension 0
- input_grad: bfloat16 [32768, 512], P(('groups', 'pos')), parts along dimension 0
- kernel_grad: float32 [1024, 5, 608], P(('groups', 'pos')), parts along dimension 0
The draws below stay inside these ranges and needn't reach their ends.
There are 2 independent parts, one for each index of `groups`. The reference program is written for one: setup_inputs(seed, part) draws one part's arguments, and reference() takes and returns one part's arrays. A program takes and returns all parts, laid end to end along the dimension named above; an argument that names none is the same for every part. Nothing has to cross between parts.
All inputs are finite; a program needn't handle non-finite values.
Results may differ from the reference program's by a relative error of at most 0.0041.
Values may be sent and summed in bfloat16 or wider, within the bound.
A program may use at most 128 MiB of HBM per device.

```python
import jax
import jax.numpy as jnp

CIN = 512
COUT = 608
KERNEL_TAPS = 5
DILATION_STEP = 4
TOKENS = 16384


def strengthened(drawn, own_key, source, target, parts, factor):
    def block_of(position):
        return (jnp.arange(drawn.shape[position]) // (drawn.shape[position] // parts)).reshape((-1,) + (1,) * (drawn.ndim - 1 - position))

    first = jax.random.permutation(own_key, parts)[block_of(target)]
    other_side = (block_of(target) + parts // 2) % parts
    return jnp.where((block_of(source) == first) | (block_of(source) == other_side), factor * drawn, drawn)


def steps_of(own_key, dims, pieces, smallest, high):
    def one(axis_at, blocks):
        steps = jax.random.uniform(jax.random.fold_in(jax.random.fold_in(own_key, 6), axis_at), (blocks,), jnp.float32, smallest / len(pieces), high / len(pieces))
        return jnp.repeat(jnp.exp(steps), dims[axis_at] // blocks).reshape((-1,) + (1,) * (len(dims) - axis_at - 1))

    loudness = one(*pieces[0])
    for cut in pieces[1:]:
        loudness = loudness * one(*cut)
    return loudness


def centred(stream_key, shape, deviation, reach, pieces=(), held_as=jnp.bfloat16):
    loudness = steps_of(stream_key, shape, pieces, -0.22, 0.18) if pieces else 1.0
    entries = jax.random.normal(stream_key, shape, jnp.float32) * deviation * loudness
    return jnp.minimum(jnp.maximum(entries, -reach), reach).astype(held_as)


def bell_draw_with(rng, extent, width, limit, shards, heavy, held_as=jnp.bfloat16):
    entries = width * jax.random.normal(rng, extent, jnp.float32)
    if shards:
        entries = entries * steps_of(rng, extent, shards, -0.22, 0.18)
    return jnp.clip(strengthened(entries, jax.random.fold_in(rng, 3), *heavy), -limit, limit).astype(held_as)


def setup_inputs(seed: int = 0, part: int = 0) -> dict:
    key_of = jax.random.split(jax.random.key(seed), 4)
    part_keys = jax.random.split(jax.random.fold_in(key_of[3], part), 4)
    return {
        "activations": bell_draw_with(part_keys[0], (TOKENS, CIN), 1.0, 6.0, ((0, 16),), (0, 1, 16, 2.0)),
        "kernel": centred(key_of[1], (CIN, KERNEL_TAPS, COUT), (CIN * KERNEL_TAPS) ** -0.5, 0.125, ((0, 16),)),
        "cotangent": centred(part_keys[2], (TOKENS // 2, COUT), 1.0, 6.0, ((0, 16),)),
    }


def gelu_value(v):
    return 0.5 * v * (1.0 + jax.scipy.special.erf(v * 0.7071067811865476))


def gelu_slope(v):
    return 0.5 * (1.0 + jax.scipy.special.erf(v * 0.7071067811865476)) + v * jnp.exp(-0.5 * v * v) * 0.3989422804014327


def reference(activations, kernel, cotangent):
    window_length = activations.shape[0]
    reach_row_count = (KERNEL_TAPS - 1) // 2 * DILATION_STEP
    values = activations.astype(jnp.float32)
    gelu = gelu_value(values).astype(jnp.bfloat16)
    padded_activation = jnp.pad(gelu, ((reach_row_count, reach_row_count), (0, 0)))
    dilated_output = jnp.zeros((window_length, kernel.shape[2]), jnp.float32)
    for tap_offset in range(KERNEL_TAPS):
        dilated_output = dilated_output + jnp.dot(padded_activation[tap_offset * DILATION_STEP:tap_offset * DILATION_STEP + window_length], kernel[:, tap_offset, :], preferred_element_type=jnp.float32)
    pooled = (0.5 * dilated_output.reshape(window_length // 2, 2, -1).sum(axis=1)).astype(jnp.bfloat16)
    convolution_gradient = (0.5 * jnp.repeat(cotangent.astype(jnp.float32), 2, axis=0)).astype(jnp.bfloat16)
    gradient_pieces = []
    for tap_offset in range(KERNEL_TAPS):
        gradient_pieces.append(jnp.dot(padded_activation[tap_offset * DILATION_STEP:tap_offset * DILATION_STEP + window_length].T, convolution_gradient, preferred_element_type=jnp.float32))
    kernel_grad = jnp.stack(gradient_pieces, axis=1)
    padded_gradient = jnp.pad(convolution_gradient, ((reach_row_count, reach_row_count), (0, 0)))
    gelu_grad = jnp.zeros((window_length, kernel.shape[0]), jnp.float32)
    for tap_offset in range(KERNEL_TAPS):
        leading_rows = (KERNEL_TAPS - 1 - tap_offset) * DILATION_STEP
        gelu_grad = gelu_grad + jnp.dot(padded_gradient[leading_rows:leading_rows + window_length], kernel[:, tap_offset, :].T, preferred_element_type=jnp.float32)
    input_grad = (gelu_grad * gelu_slope(values)).astype(jnp.bfloat16)
    return pooled, input_grad, kernel_grad
```

```python
import functools

import jax
import jax.numpy as jnp
from jax import lax
from jax.experimental import pallas as pl
from jax.experimental.pallas import tpu as pltpu
from jax.sharding import PartitionSpec as P

DILATION_STEP = 4


def extended(cells, sides, width):
    for axis, dim in sides:
        count = lax.axis_size(axis)
        ends = count - 1
        head = lax.slice_in_dim(cells, 0, width, axis=dim)
        tail = lax.slice_in_dim(cells, cells.shape[dim] - width, cells.shape[dim], axis=dim)
        cells = jnp.concatenate(
            [
                lax.ppermute(tail, axis, [(i, (i + 1) % count) for i in range(ends)]),
                cells,
                lax.ppermute(head, axis, [((i + 1) % count, i) for i in range(ends)]),
            ],
            axis=dim,
        )
    return cells


def gelu_value(v):
    return 0.5 * v * (1.0 + jax.scipy.special.erf(v * 0.7071067811865476))


def gelu_slope(v):
    return (
        0.5 * (1.0 + jax.scipy.special.erf(v * 0.7071067811865476))
        + v * jnp.exp(-0.5 * v * v) * 0.3989422804014327
    )


def on_device(activations, kernel, cotangent):
    window_length = activations.shape[0]
    kernel_taps = kernel.shape[1]
    out_width = kernel.shape[2]
    reach_row_count = (kernel_taps - 1) // 2 * DILATION_STEP
    values = activations.astype(jnp.float32)
    gelu = gelu_value(values).astype(jnp.bfloat16)
    padded_activation = extended(gelu, (("pos", 0),), reach_row_count)
    gelu_taps = jnp.stack(
        [
            padded_activation[
                tap_offset * DILATION_STEP : tap_offset * DILATION_STEP + window_length
            ]
            for tap_offset in range(kernel_taps)
        ]
    )
    kernel_full = lax.all_gather(kernel, "pos", axis=0, tiled=True)
    columns = gelu_taps
    dilated_output = jnp.einsum(
        "kpc,cko->po", columns, kernel_full, preferred_element_type=jnp.float32
    )
    pooled = (0.5 * dilated_output.reshape(window_length // 2, 2, out_width).sum(axis=1)).astype(
        jnp.bfloat16
    )
    convolution_gradient = (0.5 * jnp.repeat(cotangent.astype(jnp.float32), 2, axis=0)).astype(
        jnp.bfloat16
    )
    columns = gelu_taps
    kernel_grad = lax.psum_scatter(
        jnp.einsum(
            "kpc,po->cko", columns, convolution_gradient, preferred_element_type=jnp.float32
        ),
        "pos",
        scatter_dimension=0,
        tiled=True,
    )
    padded_gradient = extended(convolution_gradient, (("pos", 0),), reach_row_count)
    grad_taps = jnp.stack(
        [
            padded_gradient[
                (kernel_taps - 1 - tap_offset)
                * DILATION_STEP : (kernel_taps - 1 - tap_offset)
                * DILATION_STEP
                + window_length
            ]
            for tap_offset in range(kernel_taps)
        ]
    )
    block = jnp.einsum("kpo,cko->pc", grad_taps, kernel_full, preferred_element_type=jnp.float32)
    input_grad = (block * gelu_slope(values)).astype(jnp.bfloat16)
    return (pooled, input_grad, kernel_grad)


MESH = pl.DeviceIdType.MESH
F32 = jnp.float32
BF16 = jnp.bfloat16
PAD = 8


def step_kernel(
    dims,
    act, kern, cot,
    pooled, igrad, kgrad,
    weights, slope, pairs32, g2x, g2t, dx, ds, part, send1, recv1, part2, send2, recv2, send3, recv3,
    gedge, ghalo, dhalo, spread,
    own_sem, dh_s, dh_r, gh_s, gh_r,
    az_s, az_r, ay_s, ay_r, ax_s, ax_r, ac_s, ac_r,
    r1_s, r1_r, r2_s, r2_r, r3_s, r3_r,
):
    n, A, taps, rows, T2, cin, cout = dims
    step = DILATION_STEP // 2
    mid = (taps - 1) // 2
    g = lax.axis_index("groups")
    p = lax.axis_index("pos")
    c = p % 2
    y = (p // 2) % 2
    z = p // 4

    def copy(src, dst, ssem, rsem, to):
        return pltpu.make_async_remote_copy(
            src_ref=src, dst_ref=dst, send_sem=ssem, recv_sem=rsem, device_id=to, device_id_type=MESH
        )

    def at(zz, yy, cc):
        return (g, zz * 4 + yy * 2 + cc)

    core_peer, y_peer, x_peer = at(z, y, 1 - c), at(z, 1 - y, c), (1 - g, p)
    left, right = (g, (p + n - 1) % n), (g, (p + 1) % n)

    barrier = pltpu.get_barrier_semaphore()
    for d in range(1, n):
        pl.semaphore_signal(barrier, inc=1, device_id=(g, (p + d) % n), device_id_type=MESH)
    pl.semaphore_signal(barrier, inc=1, device_id=x_peer, device_id_type=MESH)
    pl.semaphore_wait(barrier, n)

    own = pltpu.make_async_copy(kern, weights.at[:, z, y, c], own_sem)
    own.start()

    dl = copy(cot.at[pl.ds(0, 16)], dhalo.at[1], dh_s.at[0], dh_r.at[1], left)
    dr = copy(cot.at[pl.ds(T2 - 16, 16)], dhalo.at[0], dh_s.at[1], dh_r.at[0], right)
    dl.start()
    dr.start()

    pending = []

    def z_gather(i):
        zz = (z + i) % A
        return copy(
            kern.at[:, g], weights.at[:, z, y, c, g], az_s.at[i], az_r.at[z], at(zz, y, c)
        )

    def y_gather(zz, src):
        return copy(src, weights.at[:, zz, y, c, g], ay_s.at[zz], ay_r.at[zz], y_peer)

    def x_gather(zz, yy):
        block = weights.at[:, zz, yy, c, g]
        return copy(block, block, ax_s.at[zz, yy], ax_r.at[zz, yy], x_peer)

    def core_gather(zz, yy, src):
        return copy(src, weights.at[:, zz, yy, c], ac_s.at[zz, yy], ac_r.at[zz, yy], core_peer)

    def go(one):
        one.start()
        pending.append(one)

    for i in range(1, A):
        go(z_gather(i))
    go(y_gather(z, kern.at[:, g]))
    go(core_gather(z, y, kern))

    tile = pairs32.shape[1]

    def gelu_tile(i, carry):
        at_row = pl.multiple_of(i * tile, tile)
        v = act[pl.ds(at_row, tile), :].astype(F32)
        e = 0.5 * (1.0 + lax.erf(v * 0.7071067811865476))
        gelu = (v * e).astype(BF16).astype(F32)
        slope[pl.ds(at_row, tile), :] = e + v * jnp.exp(-0.5 * v * v) * 0.3989422804014327
        half = pl.multiple_of(i * (tile // 2), tile // 2)
        for j in range(cin // 128):
            lanes = slice(j * 128, j * 128 + 128)
            pairs32[j] = gelu[:, lanes]
            g2x[pl.ds(PAD + half, tile // 2), lanes] = (
                pairs32[j, pl.ds(0, tile // 2, stride=2), :]
                + pairs32[j, pl.ds(1, tile // 2, stride=2), :]
            )
        return carry

    lax.fori_loop(0, 2 * T2 // tile, gelu_tile, 0)
    gedge[0] = g2x[pl.ds(PAD, 16), :].astype(BF16)
    gedge[1] = g2x[pl.ds(PAD + T2 - 16, 16), :].astype(BF16)
    gl = copy(gedge.at[0], ghalo.at[1], gh_s.at[0], gh_r.at[1], left)
    gr = copy(gedge.at[1], ghalo.at[0], gh_s.at[1], gh_r.at[0], right)
    gl.start()
    gr.start()

    cols = 128
    for i in range(cin // cols):
        g2t[pl.ds(i * cols, cols), :] = g2x[pl.ds(PAD, T2), pl.ds(i * cols, cols)].T.astype(BF16)

    keep_left = (p > 0).astype(F32)
    keep_right = (p < n - 1).astype(F32)
    for i in range(T2 // 128):
        dx[pl.ds(PAD + i * 128, 128), :] = 0.5 * cot[pl.ds(i * 128, 128), :].astype(F32)
    dl.wait_recv()
    dr.wait_recv()
    dx[pl.ds(0, PAD), :] = dhalo[0].astype(F32)[16 - PAD :] * (0.5 * keep_left)
    dx[pl.ds(PAD + T2, PAD), :] = dhalo[1].astype(F32)[:PAD] * (0.5 * keep_right)

    half_z = A // 2
    for k in range(taps):
        ds[k] = dx[pl.ds(PAD - step * (k - mid), T2), :].astype(BF16)
        for i in range(2):
            m = cin // 2
            term = jnp.dot(g2t[pl.ds(i * m, m), :], ds[k], preferred_element_type=F32)
            term = term.reshape(half_z, 2, 2, rows, cout)
            part[k, pl.ds(i * half_z, half_z)] = term
            send1[k, pl.ds(i * half_z, half_z)] = term.astype(BF16)
        go(copy(send1.at[k, :, :, 1 - c], recv1.at[k], r1_s.at[k], r1_r.at[k], core_peer))

    for k in range(taps):
        copy(send1.at[k, :, :, c], recv1.at[k], r1_s.at[k], r1_r.at[k], core_peer).wait_recv()
        for zz in range(A):
            send2[k, zz] = (part[k, zz, 1 - y, c] + recv1[k, zz, 1 - y].astype(F32)).astype(BF16)
        go(copy(send2.at[k], recv2.at[k], r2_s.at[k], r2_r.at[k], y_peer))
        for zz in range(A):
            part2[k, zz] = part[k, zz, y, c] + recv1[k, zz, y].astype(F32)

    own.wait()
    for i in range(1, A):
        zz = (z + i) % A
        got = weights.at[:, zz, y, c, g]
        copy(got, got, az_s.at[i], az_r.at[zz], at(zz, y, c)).wait_recv()
        go(y_gather(zz, got))
        go(x_gather(zz, y))

    gl.wait_recv()
    gr.wait_recv()
    g2x[pl.ds(0, PAD), :] = ghalo[0].astype(F32)[16 - PAD :] * keep_left
    g2x[pl.ds(PAD + T2, PAD), :] = ghalo[1].astype(F32)[:PAD] * keep_right

    for k in range(taps):
        copy(send2.at[k], recv2.at[k], r2_s.at[k], r2_r.at[k], y_peer).wait_recv()
        for zz in range(A):
            total = part2[k, zz] + recv2[k, zz].astype(F32)
            part2[k, zz] = total
            send3[k, zz] = total.astype(BF16)
        for i in range(1, A):
            zz = (z + i) % A
            go(copy(send3.at[k, zz], recv3.at[k, z], r3_s.at[k, i], r3_r.at[k, z], at(zz, y, c)))

    for i in range(A):
        zz = (z + i) % A
        got = weights.at[:, zz, 1 - y, c, g]
        copy(got, got, ay_s.at[zz], ay_r.at[zz], y_peer).wait_recv()
        go(x_gather(zz, 1 - y))

    for i in range(A):
        zz = (z + i) % A
        for yy in (y, 1 - y) if i else (1 - y,):
            got = weights.at[:, zz, yy, c, 1 - g]
            copy(got, got, ax_s.at[zz, yy], ax_r.at[zz, yy], x_peer).wait_recv()
            go(core_gather(zz, yy, weights.at[:, zz, yy, c]))

    for i in range(A):
        zz = (z + i) % A
        for yy in (y, 1 - y):
            got = weights.at[:, zz, yy, 1 - c]
            copy(got, got, ac_s.at[zz, yy], ac_r.at[zz, yy], core_peer).wait_recv()

    m = spread.shape[1] // 2

    def conv_tile(i, carry):
        base = pl.multiple_of(i * m, m)
        total = jnp.zeros((m, cout), F32)
        grad = jnp.zeros((m, cin), F32)
        window = g2x[pl.ds(base, m + 2 * PAD), :]
        for k in range(taps):
            off = PAD + step * (k - mid)
            w = weights[k].reshape(cin, cout)
            total += jnp.dot(
                window[off : off + m].astype(BF16), w, preferred_element_type=F32
            )
            grad += lax.dot_general(
                ds[k, pl.ds(base, m), :], w, (((1,), (1,)), ((), ())), preferred_element_type=F32
            )
        pooled[pl.ds(base, m), :] = (0.5 * total).astype(BF16)
        for j in range(cin // 128):
            lanes = slice(j * 128, j * 128 + 128)
            spread[j, pl.ds(0, m, stride=2), :] = grad[:, lanes]
            spread[j, pl.ds(1, m, stride=2), :] = grad[:, lanes]
            at_row = pl.multiple_of(i * 2 * m, 2 * m)
            igrad[pl.ds(at_row, 2 * m), lanes] = (
                spread[j] * slope[pl.ds(at_row, 2 * m), lanes]
            ).astype(BF16)
        return carry

    lax.fori_loop(0, T2 // m, conv_tile, 0)

    for k in range(taps):
        total = part2[k, z]
        for i in range(1, A):
            zz = (z + i) % A
            copy(
                send3.at[k, zz], recv3.at[k, zz], r3_s.at[k, i], r3_r.at[k, zz], at(zz, y, c)
            ).wait_recv()
            total = total + recv3[k, zz].astype(F32)
        kgrad[k] = total

    for one in (dl, dr, gl, gr):
        one.wait_send()
    for one in pending:
        one.wait_send()


def on_device_fused(activations, kernel, cotangent):
    n = lax.axis_size("pos")
    A = n // 4
    rows, taps, cout = kernel.shape
    T2 = cotangent.shape[0]
    cin = activations.shape[1]
    dims = (n, A, taps, rows, T2, cin, cout)
    kern = jnp.transpose(kernel, (1, 0, 2)).reshape(taps, 2, rows // 2, cout)
    vmem = pl.BlockSpec(memory_space=pltpu.VMEM)
    DMA = pltpu.SemaphoreType.DMA
    pooled, igrad, kgrad = pl.pallas_call(
        functools.partial(step_kernel, dims),
        out_shape=(
            jax.ShapeDtypeStruct((T2, cout), BF16),
            jax.ShapeDtypeStruct((2 * T2, cin), BF16),
            jax.ShapeDtypeStruct((taps, rows, cout), F32),
        ),
        in_specs=[vmem] * 3,
        out_specs=(vmem,) * 3,
        scratch_shapes=[
            pltpu.VMEM((taps, A, 2, 2, 2, rows // 2, cout), BF16),
            pltpu.VMEM((2 * T2, cin), F32),
            pltpu.VMEM((cin // 128, 128, 128), F32),
            pltpu.VMEM((T2 + 2 * PAD, cin), F32),
            pltpu.VMEM((cin, T2), BF16),
            pltpu.VMEM((T2 + 2 * PAD, cout), F32),
            pltpu.VMEM((taps, T2, cout), BF16),
            pltpu.VMEM((taps, A, 2, 2, rows, cout), F32),
            pltpu.VMEM((taps, A, 2, 2, rows, cout), BF16),
            pltpu.VMEM((taps, A, 2, rows, cout), BF16),
            pltpu.VMEM((taps, A, rows, cout), F32),
            pltpu.VMEM((taps, A, rows, cout), BF16),
            pltpu.VMEM((taps, A, rows, cout), BF16),
            pltpu.VMEM((taps, A, rows, cout), BF16),
            pltpu.VMEM((taps, A, rows, cout), BF16),
            pltpu.VMEM((2, 16, cin), BF16),
            pltpu.VMEM((2, 16, cin), BF16),
            pltpu.VMEM((2, 16, cout), BF16),
            pltpu.VMEM((cin // 128, 512, 128), F32),
            DMA, DMA((2,)), DMA((2,)), DMA((2,)), DMA((2,)),
            DMA((A,)), DMA((A,)), DMA((A,)), DMA((A,)),
            DMA((A, 2)), DMA((A, 2)), DMA((A, 2)), DMA((A, 2)),
            DMA((taps,)), DMA((taps,)), DMA((taps,)), DMA((taps,)),
            DMA((taps, A)), DMA((taps, A)),
        ],
        compiler_params=pltpu.CompilerParams(
            collective_id=0, has_side_effects=True, vmem_limit_bytes=50 << 20
        ),
    )(activations, kern, cotangent)
    return pooled, igrad, jnp.transpose(kgrad, (1, 0, 2))


def solution(mesh):
    placed = (P(("groups", "pos"), None), P("pos", None, None), P(("groups", "pos"), None))
    n = mesh.shape["pos"]
    fused = n == 16 and mesh.shape["groups"] == 2
    return jax.shard_map(
        on_device_fused if fused else on_device,
        mesh=mesh,
        in_specs=placed,
        out_specs=(
            P(("groups", "pos"), None),
            P(("groups", "pos"), None),
            P(("groups", "pos"), None, None),
        ),
        check_vma=False,
    )
```

```python
import functools

import jax
import jax.numpy as jnp
from jax import lax
from jax.experimental import pallas as pl
from jax.experimental.pallas import tpu as pltpu
from jax.sharding import PartitionSpec as P

DILATION_STEP = 4


def extended(cells, sides, width):
    for axis, dim in sides:
        count = lax.axis_size(axis)
        ends = count - 1
        head = lax.slice_in_dim(cells, 0, width, axis=dim)
        tail = lax.slice_in_dim(cells, cells.shape[dim] - width, cells.shape[dim], axis=dim)
        cells = jnp.concatenate(
            [
                lax.ppermute(tail, axis, [(i, (i + 1) % count) for i in range(ends)]),
                cells,
                lax.ppermute(head, axis, [((i + 1) % count, i) for i in range(ends)]),
            ],
            axis=dim,
        )
    return cells


def gelu_value(v):
    return 0.5 * v * (1.0 + jax.scipy.special.erf(v * 0.7071067811865476))


def gelu_slope(v):
    return (
        0.5 * (1.0 + jax.scipy.special.erf(v * 0.7071067811865476))
        + v * jnp.exp(-0.5 * v * v) * 0.3989422804014327
    )


def on_device(activations, kernel, cotangent):
    window_length = activations.shape[0]
    kernel_taps = kernel.shape[1]
    out_width = kernel.shape[2]
    reach_row_count = (kernel_taps - 1) // 2 * DILATION_STEP
    values = activations.astype(jnp.float32)
    gelu = gelu_value(values).astype(jnp.bfloat16)
    padded_activation = extended(gelu, (("pos", 0),), reach_row_count)
    gelu_taps = jnp.stack(
        [
            padded_activation[
                tap_offset * DILATION_STEP : tap_offset * DILATION_STEP + window_length
            ]
            for tap_offset in range(kernel_taps)
        ]
    )
    kernel_full = lax.all_gather(kernel, "pos", axis=0, tiled=True)
    columns = gelu_taps
    dilated_output = jnp.einsum(
        "kpc,cko->po", columns, kernel_full, preferred_element_type=jnp.float32
    )
    pooled = (0.5 * dilated_output.reshape(window_length // 2, 2, out_width).sum(axis=1)).astype(
        jnp.bfloat16
    )
    convolution_gradient = (0.5 * jnp.repeat(cotangent.astype(jnp.float32), 2, axis=0)).astype(
        jnp.bfloat16
    )
    columns = gelu_taps
    kernel_grad = lax.psum_scatter(
        jnp.einsum(
            "kpc,po->cko", columns, convolution_gradient, preferred_element_type=jnp.float32
        ),
        "pos",
        scatter_dimension=0,
        tiled=True,
    )
    padded_gradient = extended(convolution_gradient, (("pos", 0),), reach_row_count)
    grad_taps = jnp.stack(
        [
            padded_gradient[
                (kernel_taps - 1 - tap_offset)
                * DILATION_STEP : (kernel_taps - 1 - tap_offset)
                * DILATION_STEP
                + window_length
            ]
            for tap_offset in range(kernel_taps)
        ]
    )
    block = jnp.einsum("kpo,cko->pc", grad_taps, kernel_full, preferred_element_type=jnp.float32)
    input_grad = (block * gelu_slope(values)).astype(jnp.bfloat16)
    return (pooled, input_grad, kernel_grad)


MESH = pl.DeviceIdType.MESH
F32 = jnp.float32
BF16 = jnp.bfloat16
PAD = 8


def step_kernel(
    dims,
    act, kern, cot,
    pooled, igrad, kgrad,
    weights, slope, pairs32, g2x, g2t, dx, ds, part, send1, recv1, part2, send2, recv2, send3, recv3,
    gedge, ghalo, dhalo, spread, kout,
    own_sem, out_sem, dh_s, dh_r, gh_s, gh_r,
    az_s, az_r, ay_s, ay_r, ax_s, ax_r, ac_s, ac_r,
    r1_s, r1_r, r2_s, r2_r, r3_s, r3_r,
):
    n, A, taps, rows, T2, cin, cout = dims
    step = DILATION_STEP // 2
    mid = (taps - 1) // 2
    g = lax.axis_index("groups")
    p = lax.axis_index("pos")
    c = p % 2
    y = (p // 2) % 2
    z = p // 4

    def copy(src, dst, ssem, rsem, to):
        return pltpu.make_async_remote_copy(
            src_ref=src, dst_ref=dst, send_sem=ssem, recv_sem=rsem, device_id=to, device_id_type=MESH
        )

    def at(zz, yy, cc):
        return (g, zz * 4 + yy * 2 + cc)

    core_peer, y_peer, x_peer = at(z, y, 1 - c), at(z, 1 - y, c), (1 - g, p)
    left, right = (g, (p + n - 1) % n), (g, (p + 1) % n)

    barrier = pltpu.get_barrier_semaphore()
    for d in range(1, n):
        pl.semaphore_signal(barrier, inc=1, device_id=(g, (p + d) % n), device_id_type=MESH)
    pl.semaphore_signal(barrier, inc=1, device_id=x_peer, device_id_type=MESH)
    pl.semaphore_wait(barrier, n)

    own = pltpu.make_async_copy(kern, weights.at[:, z, y, c], own_sem)
    own.start()

    dl = copy(cot.at[pl.ds(0, 16)], dhalo.at[1], dh_s.at[0], dh_r.at[1], left)
    dr = copy(cot.at[pl.ds(T2 - 16, 16)], dhalo.at[0], dh_s.at[1], dh_r.at[0], right)
    dl.start()
    dr.start()

    pending, leaving = [], []

    high, low = z // 2, z % 2
    inner = jnp.logical_and(z > 0, z < A - 1)
    order = (z, 1 + low * (2 * high - 1), 2 + high * (1 - 2 * low), (A - 1) * (1 - high))
    onward = (None, z + 1, z - 1, (A - 1) * high)

    def partner(i):
        return order[i]

    def column(j):
        return (y, 1 - y)[j]

    def z_gather(src, zz, j, slot, to):
        yy = column(j)
        return copy(
            src, weights.at[:, zz, yy, c, g], az_s.at[slot, j], az_r.at[zz, yy], at(to, y, c)
        )

    def z_own(src, j, act_on):
        pl.when(z < A - 1)(lambda: act_on(z_gather(src, z, j, 0, z + 1)))
        pl.when(z > 0)(lambda: act_on(z_gather(src, z, j, 1, z - 1)))

    def z_onward(i, j, act_on):
        zz = partner(i)
        got = weights.at[:, zz, column(j), c, g]
        pl.when(inner)(lambda: act_on(z_gather(got, zz, j, 1 + i, onward[i])))

    def start(one):
        one.start()

    def x_gather(zz, yy):
        block = weights.at[:, zz, yy, c, g]
        return copy(block, block, ax_s.at[zz, yy], ax_r.at[zz, yy], x_peer)

    def core_gather(zz, yy, src):
        return copy(src, weights.at[:, zz, yy, c], ac_s.at[zz, yy], ac_r.at[zz, yy], core_peer)

    def go(one):
        one.start()
        pending.append(one)

    y_gather = copy(kern.at[:, g], weights.at[:, z, y, c, g], ay_s, ay_r, y_peer)
    go(y_gather)
    z_own(kern.at[:, g], 0, start)
    go(core_gather(z, y, kern))

    tile = pairs32.shape[1]

    def gelu_tile(i, carry):
        at_row = pl.multiple_of(i * tile, tile)
        v = act[pl.ds(at_row, tile), :].astype(F32)
        e = 0.5 * (1.0 + lax.erf(v * 0.7071067811865476))
        gelu = (v * e).astype(BF16).astype(F32)
        slope[pl.ds(at_row, tile), :] = e + v * jnp.exp(-0.5 * v * v) * 0.3989422804014327
        half = pl.multiple_of(i * (tile // 2), tile // 2)
        for j in range(cin // 128):
            lanes = slice(j * 128, j * 128 + 128)
            pairs32[j] = gelu[:, lanes]
            g2x[pl.ds(PAD + half, tile // 2), lanes] = (
                pairs32[j, pl.ds(0, tile // 2, stride=2), :]
                + pairs32[j, pl.ds(1, tile // 2, stride=2), :]
            )
        return carry

    lax.fori_loop(0, 2 * T2 // tile, gelu_tile, 0)
    gedge[0] = g2x[pl.ds(PAD, 16), :].astype(BF16)
    gedge[1] = g2x[pl.ds(PAD + T2 - 16, 16), :].astype(BF16)
    gl = copy(gedge.at[0], ghalo.at[1], gh_s.at[0], gh_r.at[1], left)
    gr = copy(gedge.at[1], ghalo.at[0], gh_s.at[1], gh_r.at[0], right)
    gl.start()
    gr.start()


    def take_z(i, j):
        zz, yy = partner(i), column(j)
        got = weights.at[:, zz, yy, c, g]
        copy(got, got, az_s.at[1 + i, j], az_r.at[zz, yy], y_peer).wait_recv()
        z_onward(i, j, start)
        go(x_gather(zz, yy))

    def take_x(i, yy):
        zz = partner(i)
        got = weights.at[:, zz, yy, c, 1 - g]
        copy(got, got, ax_s.at[zz, yy], ax_r.at[zz, yy], x_peer).wait_recv()
        go(core_gather(zz, yy, weights.at[:, zz, yy, c]))

    def take_core(i, yy):
        zz = partner(i)
        got = weights.at[:, zz, yy, 1 - c]
        copy(got, got, ac_s.at[zz, yy], ac_r.at[zz, yy], core_peer).wait_recv()

    def tap_dot(k):
        ds[k] = dx[pl.ds(PAD - step * (k - mid), T2), :].astype(BF16)
        half_z = A // 2
        for i in range(2):
            m = cin // 2
            term = jnp.dot(g2t[pl.ds(i * m, m), :], ds[k], preferred_element_type=F32)
            term = term.reshape(half_z, 2, 2, rows, cout)
            part[k, pl.ds(i * half_z, half_z)] = term
            send1[k, pl.ds(i * half_z, half_z)] = term.astype(BF16)
        go(copy(send1.at[k, :, :, 1 - c], recv1.at[k], r1_s.at[k], r1_r.at[k], core_peer))

    def tap_core(k):
        copy(send1.at[k, :, :, c], recv1.at[k], r1_s.at[k], r1_r.at[k], core_peer).wait_recv()
        for zz in range(A):
            send2[k, zz] = (part[k, zz, 1 - y, c] + recv1[k, zz, 1 - y].astype(F32)).astype(BF16)
        go(copy(send2.at[k], recv2.at[k], r2_s.at[k], r2_r.at[k], y_peer))
        for zz in range(A):
            part2[k, zz] = part[k, zz, y, c] + recv1[k, zz, y].astype(F32)

    def tap_y(k):
        copy(send2.at[k], recv2.at[k], r2_s.at[k], r2_r.at[k], y_peer).wait_recv()
        for zz in range(A):
            total = part2[k, zz] + recv2[k, zz].astype(F32)
            part2[k, zz] = total
            send3[k, zz] = total.astype(BF16)
        for i in range(1, A):
            zz = partner(i)
            go(copy(send3.at[k, zz], recv3.at[k, z], r3_s.at[k, i], r3_r.at[k, z], at(zz, y, c)))

    def tap_z(k):
        total = part2[k, z]
        for i in range(1, A):
            zz = partner(i)
            copy(
                send3.at[k, zz], recv3.at[k, zz], r3_s.at[k, i], r3_r.at[k, zz], at(zz, y, c)
            ).wait_recv()
            total = total + recv3[k, zz].astype(F32)
        kout[k] = total
        done = pltpu.make_async_copy(kout.at[k], kgrad.at[k], out_sem.at[k])
        done.start()
        leaving.append(done)

    own.wait()
    y_gather.wait_recv()
    across = weights.at[:, z, 1 - y, c, g]
    z_own(across, 1, start)
    go(x_gather(z, 1 - y))
    take_z(1, 0)
    cols = 128
    for i in range(cin // cols):
        g2t[pl.ds(i * cols, cols), :] = g2x[pl.ds(PAD, T2), pl.ds(i * cols, cols)].T.astype(BF16)

    keep_left = (p > 0).astype(F32)
    keep_right = (p < n - 1).astype(F32)
    for i in range(T2 // 128):
        dx[pl.ds(PAD + i * 128, 128), :] = 0.5 * cot[pl.ds(i * 128, 128), :].astype(F32)
    dl.wait_recv()
    dr.wait_recv()
    dx[pl.ds(0, PAD), :] = dhalo[0].astype(F32)[16 - PAD :] * (0.5 * keep_left)
    dx[pl.ds(PAD + T2, PAD), :] = dhalo[1].astype(F32)[:PAD] * (0.5 * keep_right)


    arrivals = ((1, 1), (2, 0), (2, 1), (3, 0))
    for k in range(taps):
        tap_dot(k)
        if k:
            tap_core(k - 1)
        if k < len(arrivals):
            take_z(*arrivals[k])
    tap_core(taps - 1)
    take_z(3, 1)
    gl.wait_recv()
    gr.wait_recv()
    g2x[pl.ds(0, PAD), :] = ghalo[0].astype(F32)[16 - PAD :] * keep_left
    g2x[pl.ds(PAD + T2, PAD), :] = ghalo[1].astype(F32)[:PAD] * keep_right
    take_x(0, 1 - y)
    take_x(1, y)
    take_x(1, 1 - y)
    tap_y(0)
    take_x(2, y)
    take_x(2, 1 - y)
    tap_y(1)
    take_x(3, y)
    take_x(3, 1 - y)
    tap_y(2)
    for i in range(A):
        take_core(i, y)
        take_core(i, 1 - y)

    m = spread.shape[1] // 2

    def conv_tile(i, carry):
        base = pl.multiple_of(i * m, m)
        total = jnp.zeros((m, cout), F32)
        grad = jnp.zeros((m, cin), F32)
        window = g2x[pl.ds(base, m + 2 * PAD), :]
        for k in range(taps):
            off = PAD + step * (k - mid)
            w = weights[k].reshape(cin, cout)
            total += jnp.dot(
                window[off : off + m].astype(BF16), w, preferred_element_type=F32
            )
            grad += lax.dot_general(
                ds[k, pl.ds(base, m), :], w, (((1,), (1,)), ((), ())), preferred_element_type=F32
            )
        pooled[pl.ds(base, m), :] = (0.5 * total).astype(BF16)
        for j in range(cin // 128):
            lanes = slice(j * 128, j * 128 + 128)
            spread[j, pl.ds(0, m, stride=2), :] = grad[:, lanes]
            spread[j, pl.ds(1, m, stride=2), :] = grad[:, lanes]
            at_row = pl.multiple_of(i * 2 * m, 2 * m)
            igrad[pl.ds(at_row, 2 * m), lanes] = (
                spread[j] * slope[pl.ds(at_row, 2 * m), lanes]
            ).astype(BF16)
        return carry

    lax.fori_loop(0, T2 // m, conv_tile, 0)

    for k in range(3, taps):
        tap_y(k)
    for k in range(taps):
        tap_z(k)

    for one in leaving:
        one.wait()
    for one in (dl, dr, gl, gr):
        one.wait_send()
    for one in pending:
        one.wait_send()
    z_own(kern.at[:, g], 0, lambda one: one.wait_send())
    z_own(across, 1, lambda one: one.wait_send())
    for i in range(1, A):
        for j in range(2):
            z_onward(i, j, lambda one: one.wait_send())


def on_device_fused(activations, kernel, cotangent):
    n = lax.axis_size("pos")
    A = n // 4
    rows, taps, cout = kernel.shape
    T2 = cotangent.shape[0]
    cin = activations.shape[1]
    dims = (n, A, taps, rows, T2, cin, cout)
    kern = jnp.transpose(kernel, (1, 0, 2)).reshape(taps, 2, rows // 2, cout)
    vmem = pl.BlockSpec(memory_space=pltpu.VMEM)
    DMA = pltpu.SemaphoreType.DMA
    pooled, igrad, kgrad = pl.pallas_call(
        functools.partial(step_kernel, dims),
        out_shape=(
            jax.ShapeDtypeStruct((T2, cout), BF16),
            jax.ShapeDtypeStruct((2 * T2, cin), BF16),
            jax.ShapeDtypeStruct((taps, rows, cout), F32),
        ),
        in_specs=[vmem, pl.BlockSpec(memory_space=pltpu.HBM), vmem],
        out_specs=(vmem, vmem, pl.BlockSpec(memory_space=pltpu.HBM)),
        scratch_shapes=[
            pltpu.VMEM((taps, A, 2, 2, 2, rows // 2, cout), BF16),
            pltpu.VMEM((2 * T2, cin), F32),
            pltpu.VMEM((cin // 128, 128, 128), F32),
            pltpu.VMEM((T2 + 2 * PAD, cin), F32),
            pltpu.VMEM((cin, T2), BF16),
            pltpu.VMEM((T2 + 2 * PAD, cout), F32),
            pltpu.VMEM((taps, T2, cout), BF16),
            pltpu.VMEM((taps, A, 2, 2, rows, cout), F32),
            pltpu.VMEM((taps, A, 2, 2, rows, cout), BF16),
            pltpu.VMEM((taps, A, 2, rows, cout), BF16),
            pltpu.VMEM((taps, A, rows, cout), F32),
            pltpu.VMEM((taps, A, rows, cout), BF16),
            pltpu.VMEM((taps, A, rows, cout), BF16),
            pltpu.VMEM((taps, A, rows, cout), BF16),
            pltpu.VMEM((taps, A, rows, cout), BF16),
            pltpu.VMEM((2, 16, cin), BF16),
            pltpu.VMEM((2, 16, cin), BF16),
            pltpu.VMEM((2, 16, cout), BF16),
            pltpu.VMEM((cin // 128, 512, 128), F32),
            pltpu.VMEM((taps, rows, cout), F32),
            DMA, DMA((taps,)), DMA((2,)), DMA((2,)), DMA((2,)), DMA((2,)),
            DMA((A + 1, 2)), DMA((A, 2)), DMA, DMA,
            DMA((A, 2)), DMA((A, 2)), DMA((A, 2)), DMA((A, 2)),
            DMA((taps,)), DMA((taps,)), DMA((taps,)), DMA((taps,)),
            DMA((taps, A)), DMA((taps, A)),
        ],
        compiler_params=pltpu.CompilerParams(
            collective_id=0, has_side_effects=True, vmem_limit_bytes=50 << 20
        ),
    )(activations, kern, cotangent)
    return pooled, igrad, jnp.transpose(kgrad, (1, 0, 2))


def solution(mesh):
    placed = (P(("groups", "pos"), None), P("pos", None, None), P(("groups", "pos"), None))
    n = mesh.shape["pos"]
    fused = n == 16 and mesh.shape["groups"] == 2
    return jax.shard_map(
        on_device_fused if fused else on_device,
        mesh=mesh,
        in_specs=placed,
        out_specs=(
            P(("groups", "pos"), None),
            P(("groups", "pos"), None),
            P(("groups", "pos"), None, None),
        ),
        check_vma=False,
    )
```

```python
import functools

import jax
import jax.numpy as jnp
from jax import lax
from jax.experimental import pallas as pl
from jax.experimental.pallas import tpu as pltpu
from jax.sharding import PartitionSpec as P

DILATION_STEP = 4


def extended(cells, sides, width):
    for axis, dim in sides:
        count = lax.axis_size(axis)
        ends = count - 1
        head = lax.slice_in_dim(cells, 0, width, axis=dim)
        tail = lax.slice_in_dim(cells, cells.shape[dim] - width, cells.shape[dim], axis=dim)
        cells = jnp.concatenate(
            [
                lax.ppermute(tail, axis, [(i, (i + 1) % count) for i in range(ends)]),
                cells,
                lax.ppermute(head, axis, [((i + 1) % count, i) for i in range(ends)]),
            ],
            axis=dim,
        )
    return cells


def gelu_value(v):
    return 0.5 * v * (1.0 + jax.scipy.special.erf(v * 0.7071067811865476))


def gelu_slope(v):
    return (
        0.5 * (1.0 + jax.scipy.special.erf(v * 0.7071067811865476))
        + v * jnp.exp(-0.5 * v * v) * 0.3989422804014327
    )


def on_device(activations, kernel, cotangent):
    window_length = activations.shape[0]
    kernel_taps = kernel.shape[1]
    out_width = kernel.shape[2]
    reach_row_count = (kernel_taps - 1) // 2 * DILATION_STEP
    values = activations.astype(jnp.float32)
    gelu = gelu_value(values).astype(jnp.bfloat16)
    padded_activation = extended(gelu, (("pos", 0),), reach_row_count)
    gelu_taps = jnp.stack(
        [
            padded_activation[
                tap_offset * DILATION_STEP : tap_offset * DILATION_STEP + window_length
            ]
            for tap_offset in range(kernel_taps)
        ]
    )
    kernel_full = lax.all_gather(kernel, "pos", axis=0, tiled=True)
    columns = gelu_taps
    dilated_output = jnp.einsum(
        "kpc,cko->po", columns, kernel_full, preferred_element_type=jnp.float32
    )
    pooled = (0.5 * dilated_output.reshape(window_length // 2, 2, out_width).sum(axis=1)).astype(
        jnp.bfloat16
    )
    convolution_gradient = (0.5 * jnp.repeat(cotangent.astype(jnp.float32), 2, axis=0)).astype(
        jnp.bfloat16
    )
    columns = gelu_taps
    kernel_grad = lax.psum_scatter(
        jnp.einsum(
            "kpc,po->cko", columns, convolution_gradient, preferred_element_type=jnp.float32
        ),
        "pos",
        scatter_dimension=0,
        tiled=True,
    )
    padded_gradient = extended(convolution_gradient, (("pos", 0),), reach_row_count)
    grad_taps = jnp.stack(
        [
            padded_gradient[
                (kernel_taps - 1 - tap_offset)
                * DILATION_STEP : (kernel_taps - 1 - tap_offset)
                * DILATION_STEP
                + window_length
            ]
            for tap_offset in range(kernel_taps)
        ]
    )
    block = jnp.einsum("kpo,cko->pc", grad_taps, kernel_full, preferred_element_type=jnp.float32)
    input_grad = (block * gelu_slope(values)).astype(jnp.bfloat16)
    return (pooled, input_grad, kernel_grad)


MESH = pl.DeviceIdType.MESH
F32 = jnp.float32
BF16 = jnp.bfloat16
PAD = 8


def step_kernel(
    dims,
    act, kern, cot,
    pooled, igrad, kgrad,
    weights, slope, pairs32, g2x, g2t, dx, ds, part, send1, recv1, part2, send2, recv2, send3, recv3,
    gedge, ghalo, dhalo, spread, kout,
    own_sem, out_sem, dh_s, dh_r, gh_s, gh_r,
    az_s, az_r, ay_s, ay_r, ax_s, ax_r, ac_s, ac_r,
    r1_s, r1_r, r2_s, r2_r, r3_s, r3_r,
):
    n, A, taps, rows, T2, cin, cout = dims
    step = DILATION_STEP // 2
    mid = (taps - 1) // 2
    g = lax.axis_index("groups")
    p = lax.axis_index("pos")
    c = p % 2
    y = (p // 2) % 2
    z = p // 4

    def copy(src, dst, ssem, rsem, to):
        return pltpu.make_async_remote_copy(
            src_ref=src, dst_ref=dst, send_sem=ssem, recv_sem=rsem, device_id=to, device_id_type=MESH
        )

    def at(zz, yy, cc):
        return (g, zz * 4 + yy * 2 + cc)

    core_peer, y_peer, x_peer = at(z, y, 1 - c), at(z, 1 - y, c), (1 - g, p)
    left, right = (g, (p + n - 1) % n), (g, (p + 1) % n)

    barrier = pltpu.get_barrier_semaphore()
    for d in range(1, n):
        pl.semaphore_signal(barrier, inc=1, device_id=(g, (p + d) % n), device_id_type=MESH)
    pl.semaphore_signal(barrier, inc=1, device_id=x_peer, device_id_type=MESH)
    pl.semaphore_wait(barrier, n)

    own = pltpu.make_async_copy(kern, weights.at[:, z, y, c], own_sem)
    own.start()

    dl = copy(cot.at[pl.ds(0, 16)], dhalo.at[1], dh_s.at[0], dh_r.at[1], left)
    dr = copy(cot.at[pl.ds(T2 - 16, 16)], dhalo.at[0], dh_s.at[1], dh_r.at[0], right)
    dl.start()
    dr.start()

    pending, leaving = [], []

    high, low = z // 2, z % 2
    inner = jnp.logical_and(z > 0, z < A - 1)
    order = (z, 1 + low * (2 * high - 1), 2 + high * (1 - 2 * low), (A - 1) * (1 - high))
    onward = (None, z + 1, z - 1, (A - 1) * high)

    def partner(i):
        return order[i]

    def column(j):
        return (y, 1 - y)[j]

    def z_gather(src, zz, j, slot, to):
        yy = column(j)
        return copy(
            src, weights.at[:, zz, yy, c, g], az_s.at[slot, j], az_r.at[zz, yy], at(to, y, c)
        )

    def z_own(src, j, act_on):
        pl.when(z < A - 1)(lambda: act_on(z_gather(src, z, j, 0, z + 1)))
        pl.when(z > 0)(lambda: act_on(z_gather(src, z, j, 1, z - 1)))

    def z_onward(i, j, act_on):
        zz = partner(i)
        got = weights.at[:, zz, column(j), c, g]
        pl.when(inner)(lambda: act_on(z_gather(got, zz, j, 1 + i, onward[i])))

    def start(one):
        one.start()

    def x_gather(zz, yy):
        block = weights.at[:, zz, yy, c, g]
        return copy(block, block, ax_s.at[zz, yy], ax_r.at[zz, yy], x_peer)

    def core_gather(zz, yy, src):
        return copy(src, weights.at[:, zz, yy, c], ac_s.at[zz, yy], ac_r.at[zz, yy], core_peer)

    def go(one):
        one.start()
        pending.append(one)

    y_gather = copy(kern.at[:, g], weights.at[:, z, y, c, g], ay_s, ay_r, y_peer)
    go(y_gather)
    z_own(kern.at[:, g], 0, start)
    go(core_gather(z, y, kern))

    tile = pairs32.shape[1]

    def gelu_tile(i, carry):
        at_row = pl.multiple_of(i * tile, tile)
        v = act[pl.ds(at_row, tile), :].astype(F32)
        e = 0.5 * (1.0 + lax.erf(v * 0.7071067811865476))
        gelu = (v * e).astype(BF16).astype(F32)
        slope[pl.ds(at_row, tile), :] = e + v * jnp.exp(-0.5 * v * v) * 0.3989422804014327
        half = pl.multiple_of(i * (tile // 2), tile // 2)
        for j in range(cin // 128):
            lanes = slice(j * 128, j * 128 + 128)
            pairs32[j] = gelu[:, lanes]
            g2x[pl.ds(PAD + half, tile // 2), lanes] = (
                pairs32[j, pl.ds(0, tile // 2, stride=2), :]
                + pairs32[j, pl.ds(1, tile // 2, stride=2), :]
            )
        return carry

    lax.fori_loop(0, 2 * T2 // tile, gelu_tile, 0)
    gedge[0] = g2x[pl.ds(PAD, 16), :].astype(BF16)
    gedge[1] = g2x[pl.ds(PAD + T2 - 16, 16), :].astype(BF16)
    gl = copy(gedge.at[0], ghalo.at[1], gh_s.at[0], gh_r.at[1], left)
    gr = copy(gedge.at[1], ghalo.at[0], gh_s.at[1], gh_r.at[0], right)
    gl.start()
    gr.start()


    def take_z(i, j):
        zz, yy = partner(i), column(j)
        got = weights.at[:, zz, yy, c, g]
        copy(got, got, az_s.at[1 + i, j], az_r.at[zz, yy], y_peer).wait_recv()
        z_onward(i, j, start)
        go(x_gather(zz, yy))

    def take_x(i, yy):
        zz = partner(i)
        got = weights.at[:, zz, yy, c, 1 - g]
        copy(got, got, ax_s.at[zz, yy], ax_r.at[zz, yy], x_peer).wait_recv()
        go(core_gather(zz, yy, weights.at[:, zz, yy, c]))

    def take_core(i, yy):
        zz = partner(i)
        got = weights.at[:, zz, yy, 1 - c]
        copy(got, got, ac_s.at[zz, yy], ac_r.at[zz, yy], core_peer).wait_recv()

    def tap_dot(k):
        ds[k] = dx[pl.ds(PAD - step * (k - mid), T2), :].astype(BF16)
        half_z = A // 2
        for i in range(2):
            m = cin // 2
            term = jnp.dot(g2t[pl.ds(i * m, m), :], ds[k], preferred_element_type=F32)
            term = term.reshape(half_z, 2, 2, rows, cout)
            part[k, pl.ds(i * half_z, half_z)] = term
            send1[k, pl.ds(i * half_z, half_z)] = term.astype(BF16)
        go(copy(send1.at[k, :, :, 1 - c], recv1.at[k], r1_s.at[k], r1_r.at[k], core_peer))

    def tap_core(k):
        copy(send1.at[k, :, :, c], recv1.at[k], r1_s.at[k], r1_r.at[k], core_peer).wait_recv()
        for zz in range(A):
            send2[k, zz] = (part[k, zz, 1 - y, c] + recv1[k, zz, 1 - y].astype(F32)).astype(BF16)
        go(copy(send2.at[k], recv2.at[k], r2_s.at[k], r2_r.at[k], y_peer))
        for zz in range(A):
            part2[k, zz] = part[k, zz, y, c] + recv1[k, zz, y].astype(F32)

    def tap_y(k):
        copy(send2.at[k], recv2.at[k], r2_s.at[k], r2_r.at[k], y_peer).wait_recv()
        for zz in range(A):
            total = part2[k, zz] + recv2[k, zz].astype(F32)
            part2[k, zz] = total
            send3[k, zz] = total.astype(BF16)
        for i in range(1, A):
            zz = partner(i)
            go(copy(send3.at[k, zz], recv3.at[k, z], r3_s.at[k, i], r3_r.at[k, z], at(zz, y, c)))

    def tap_z(k):
        total = part2[k, z]
        for i in range(1, A):
            zz = partner(i)
            copy(
                send3.at[k, zz], recv3.at[k, zz], r3_s.at[k, i], r3_r.at[k, zz], at(zz, y, c)
            ).wait_recv()
            total = total + recv3[k, zz].astype(F32)
        kout[k] = total
        done = pltpu.make_async_copy(kout.at[k], kgrad.at[k], out_sem.at[k])
        done.start()
        leaving.append(done)

    own.wait()
    y_gather.wait_recv()
    across = weights.at[:, z, 1 - y, c, g]
    z_own(across, 1, start)
    go(x_gather(z, 1 - y))
    take_z(1, 0)
    cols = 128
    for i in range(cin // cols):
        g2t[pl.ds(i * cols, cols), :] = g2x[pl.ds(PAD, T2), pl.ds(i * cols, cols)].T.astype(BF16)

    keep_left = (p > 0).astype(F32)
    keep_right = (p < n - 1).astype(F32)
    for i in range(T2 // 128):
        dx[pl.ds(PAD + i * 128, 128), :] = 0.5 * cot[pl.ds(i * 128, 128), :].astype(F32)
    dl.wait_recv()
    dr.wait_recv()
    dx[pl.ds(0, PAD), :] = dhalo[0].astype(F32)[16 - PAD :] * (0.5 * keep_left)
    dx[pl.ds(PAD + T2, PAD), :] = dhalo[1].astype(F32)[:PAD] * (0.5 * keep_right)


    arrivals = ((1, 1), (2, 0), (2, 1), (3, 0))
    for k in range(taps):
        tap_dot(k)
        if k:
            tap_core(k - 1)
        if k < len(arrivals):
            take_z(*arrivals[k])
    tap_core(taps - 1)
    take_z(3, 1)
    gl.wait_recv()
    gr.wait_recv()
    g2x[pl.ds(0, PAD), :] = ghalo[0].astype(F32)[16 - PAD :] * keep_left
    g2x[pl.ds(PAD + T2, PAD), :] = ghalo[1].astype(F32)[:PAD] * keep_right
    take_x(0, 1 - y)
    take_x(1, y)
    take_x(1, 1 - y)
    tap_y(0)
    take_x(2, y)
    take_x(2, 1 - y)
    tap_y(1)
    take_x(3, y)
    take_x(3, 1 - y)
    for k in range(2, taps - 1):
        tap_y(k)
    for i in range(A):
        take_core(i, y)
        take_core(i, 1 - y)

    m = spread.shape[1] // 2

    def conv_tile(i, carry):
        base = pl.multiple_of(i * m, m)
        total = jnp.zeros((m, cout), F32)
        grad = jnp.zeros((m, cin), F32)
        window = g2x[pl.ds(base, m + 2 * PAD), :]
        for k in range(taps):
            off = PAD + step * (k - mid)
            w = weights[k].reshape(cin, cout)
            total += jnp.dot(
                window[off : off + m].astype(BF16), w, preferred_element_type=F32
            )
            grad += lax.dot_general(
                ds[k, pl.ds(base, m), :], w, (((1,), (1,)), ((), ())), preferred_element_type=F32
            )
        pooled[pl.ds(base, m), :] = (0.5 * total).astype(BF16)
        for j in range(cin // 128):
            lanes = slice(j * 128, j * 128 + 128)
            spread[j, pl.ds(0, m, stride=2), :] = grad[:, lanes]
            spread[j, pl.ds(1, m, stride=2), :] = grad[:, lanes]
            at_row = pl.multiple_of(i * 2 * m, 2 * m)
            igrad[pl.ds(at_row, 2 * m), lanes] = (
                spread[j] * slope[pl.ds(at_row, 2 * m), lanes]
            ).astype(BF16)
        return carry

    lax.fori_loop(0, 1, conv_tile, 0)
    tap_y(taps - 1)
    lax.fori_loop(1, T2 // m, conv_tile, 0)

    for k in range(taps):
        tap_z(k)

    for one in leaving:
        one.wait()
    for one in (dl, dr, gl, gr):
        one.wait_send()
    for one in pending:
        one.wait_send()
    z_own(kern.at[:, g], 0, lambda one: one.wait_send())
    z_own(across, 1, lambda one: one.wait_send())
    for i in range(1, A):
        for j in range(2):
            z_onward(i, j, lambda one: one.wait_send())


def on_device_fused(activations, kernel, cotangent):
    n = lax.axis_size("pos")
    A = n // 4
    rows, taps, cout = kernel.shape
    T2 = cotangent.shape[0]
    cin = activations.shape[1]
    dims = (n, A, taps, rows, T2, cin, cout)
    kern = jnp.transpose(kernel, (1, 0, 2)).reshape(taps, 2, rows // 2, cout)
    vmem = pl.BlockSpec(memory_space=pltpu.VMEM)
    DMA = pltpu.SemaphoreType.DMA
    pooled, igrad, kgrad = pl.pallas_call(
        functools.partial(step_kernel, dims),
        out_shape=(
            jax.ShapeDtypeStruct((T2, cout), BF16),
            jax.ShapeDtypeStruct((2 * T2, cin), BF16),
            jax.ShapeDtypeStruct((taps, rows, cout), F32),
        ),
        in_specs=[vmem, pl.BlockSpec(memory_space=pltpu.HBM), vmem],
        out_specs=(vmem, vmem, pl.BlockSpec(memory_space=pltpu.HBM)),
        scratch_shapes=[
            pltpu.VMEM((taps, A, 2, 2, 2, rows // 2, cout), BF16),
            pltpu.VMEM((2 * T2, cin), F32),
            pltpu.VMEM((cin // 128, 128, 128), F32),
            pltpu.VMEM((T2 + 2 * PAD, cin), F32),
            pltpu.VMEM((cin, T2), BF16),
            pltpu.VMEM((T2 + 2 * PAD, cout), F32),
            pltpu.VMEM((taps, T2, cout), BF16),
            pltpu.VMEM((taps, A, 2, 2, rows, cout), F32),
            pltpu.VMEM((taps, A, 2, 2, rows, cout), BF16),
            pltpu.VMEM((taps, A, 2, rows, cout), BF16),
            pltpu.VMEM((taps, A, rows, cout), F32),
            pltpu.VMEM((taps, A, rows, cout), BF16),
            pltpu.VMEM((taps, A, rows, cout), BF16),
            pltpu.VMEM((taps, A, rows, cout), BF16),
            pltpu.VMEM((taps, A, rows, cout), BF16),
            pltpu.VMEM((2, 16, cin), BF16),
            pltpu.VMEM((2, 16, cin), BF16),
            pltpu.VMEM((2, 16, cout), BF16),
            pltpu.VMEM((cin // 128, 512, 128), F32),
            pltpu.VMEM((taps, rows, cout), F32),
            DMA, DMA((taps,)), DMA((2,)), DMA((2,)), DMA((2,)), DMA((2,)),
            DMA((A + 1, 2)), DMA((A, 2)), DMA, DMA,
            DMA((A, 2)), DMA((A, 2)), DMA((A, 2)), DMA((A, 2)),
            DMA((taps,)), DMA((taps,)), DMA((taps,)), DMA((taps,)),
            DMA((taps, A)), DMA((taps, A)),
        ],
        compiler_params=pltpu.CompilerParams(
            collective_id=0, has_side_effects=True, vmem_limit_bytes=50 << 20
        ),
    )(activations, kern, cotangent)
    return pooled, igrad, jnp.transpose(kgrad, (1, 0, 2))


def solution(mesh):
    placed = (P(("groups", "pos"), None), P("pos", None, None), P(("groups", "pos"), None))
    n = mesh.shape["pos"]
    fused = n == 16 and mesh.shape["groups"] == 2
    return jax.shard_map(
        on_device_fused if fused else on_device,
        mesh=mesh,
        in_specs=placed,
        out_specs=(
            P(("groups", "pos"), None),
            P(("groups", "pos"), None),
            P(("groups", "pos"), None, None),
        ),
        check_vma=False,
    )
```

```python
import functools

import jax
import jax.numpy as jnp
from jax import lax
from jax.experimental import pallas as pl
from jax.experimental.pallas import tpu as pltpu
from jax.sharding import PartitionSpec as P

DILATION_STEP = 4


def extended(cells, sides, width):
    for axis, dim in sides:
        count = lax.axis_size(axis)
        ends = count - 1
        head = lax.slice_in_dim(cells, 0, width, axis=dim)
        tail = lax.slice_in_dim(cells, cells.shape[dim] - width, cells.shape[dim], axis=dim)
        cells = jnp.concatenate(
            [
                lax.ppermute(tail, axis, [(i, (i + 1) % count) for i in range(ends)]),
                cells,
                lax.ppermute(head, axis, [((i + 1) % count, i) for i in range(ends)]),
            ],
            axis=dim,
        )
    return cells


def gelu_value(v):
    return 0.5 * v * (1.0 + jax.scipy.special.erf(v * 0.7071067811865476))


def gelu_slope(v):
    return (
        0.5 * (1.0 + jax.scipy.special.erf(v * 0.7071067811865476))
        + v * jnp.exp(-0.5 * v * v) * 0.3989422804014327
    )


def on_device(activations, kernel, cotangent):
    window_length = activations.shape[0]
    kernel_taps = kernel.shape[1]
    out_width = kernel.shape[2]
    reach_row_count = (kernel_taps - 1) // 2 * DILATION_STEP
    values = activations.astype(jnp.float32)
    gelu = gelu_value(values).astype(jnp.bfloat16)
    padded_activation = extended(gelu, (("pos", 0),), reach_row_count)
    gelu_taps = jnp.stack(
        [
            padded_activation[
                tap_offset * DILATION_STEP : tap_offset * DILATION_STEP + window_length
            ]
            for tap_offset in range(kernel_taps)
        ]
    )
    kernel_full = lax.all_gather(kernel, "pos", axis=0, tiled=True)
    columns = gelu_taps
    dilated_output = jnp.einsum(
        "kpc,cko->po", columns, kernel_full, preferred_element_type=jnp.float32
    )
    pooled = (0.5 * dilated_output.reshape(window_length // 2, 2, out_width).sum(axis=1)).astype(
        jnp.bfloat16
    )
    convolution_gradient = (0.5 * jnp.repeat(cotangent.astype(jnp.float32), 2, axis=0)).astype(
        jnp.bfloat16
    )
    columns = gelu_taps
    kernel_grad = lax.psum_scatter(
        jnp.einsum(
            "kpc,po->cko", columns, convolution_gradient, preferred_element_type=jnp.float32
        ),
        "pos",
        scatter_dimension=0,
        tiled=True,
    )
    padded_gradient = extended(convolution_gradient, (("pos", 0),), reach_row_count)
    grad_taps = jnp.stack(
        [
            padded_gradient[
                (kernel_taps - 1 - tap_offset)
                * DILATION_STEP : (kernel_taps - 1 - tap_offset)
                * DILATION_STEP
                + window_length
            ]
            for tap_offset in range(kernel_taps)
        ]
    )
    block = jnp.einsum("kpo,cko->pc", grad_taps, kernel_full, preferred_element_type=jnp.float32)
    input_grad = (block * gelu_slope(values)).astype(jnp.bfloat16)
    return (pooled, input_grad, kernel_grad)


MESH = pl.DeviceIdType.MESH
F32 = jnp.float32
BF16 = jnp.bfloat16
PAD = 8


def step_kernel(
    dims,
    act, kern, cot,
    pooled, igrad, kgrad,
    weights, slope, pairs32, g2x, g2t, dx, ds, part, send1, recv1, part2, send2, recv2, send3, recv3,
    gedge, ghalo, dhalo, spread, kout,
    own_sem, out_sem, dh_s, dh_r, gh_s, gh_r,
    az_s, az_r, ay_s, ay_r, ax_s, ax_r, ac_s, ac_r,
    r1_s, r1_r, r2_s, r2_r, r3_s, r3_r,
):
    n, A, taps, rows, T2, cin, cout = dims
    step = DILATION_STEP // 2
    mid = (taps - 1) // 2
    g = lax.axis_index("groups")
    p = lax.axis_index("pos")
    c = p % 2
    y = (p // 2) % 2
    z = p // 4

    def copy(src, dst, ssem, rsem, to):
        return pltpu.make_async_remote_copy(
            src_ref=src, dst_ref=dst, send_sem=ssem, recv_sem=rsem, device_id=to, device_id_type=MESH
        )

    def at(zz, yy, cc):
        return (g, zz * 4 + yy * 2 + cc)

    core_peer, y_peer, x_peer = at(z, y, 1 - c), at(z, 1 - y, c), (1 - g, p)
    left, right = (g, (p + n - 1) % n), (g, (p + 1) % n)

    barrier = pltpu.get_barrier_semaphore()
    for d in range(1, n):
        pl.semaphore_signal(barrier, inc=1, device_id=(g, (p + d) % n), device_id_type=MESH)
    pl.semaphore_signal(barrier, inc=1, device_id=x_peer, device_id_type=MESH)
    pl.semaphore_wait(barrier, n)

    own = pltpu.make_async_copy(kern, weights.at[:, z, y, c], own_sem)
    own.start()

    dl = copy(cot.at[pl.ds(0, 16)], dhalo.at[1], dh_s.at[0], dh_r.at[1], left)
    dr = copy(cot.at[pl.ds(T2 - 16, 16)], dhalo.at[0], dh_s.at[1], dh_r.at[0], right)
    dl.start()
    dr.start()

    pending, leaving = [], []

    high, low = z // 2, z % 2
    inner = jnp.logical_and(z > 0, z < A - 1)
    order = (z, 1 + low * (2 * high - 1), 2 + high * (1 - 2 * low), (A - 1) * (1 - high))
    onward = (None, z + 1, z - 1, (A - 1) * high)

    def partner(i):
        return order[i]

    def column(j):
        return (y, 1 - y)[j]

    def z_gather(src, zz, j, slot, to):
        yy = column(j)
        return copy(
            src, weights.at[:, zz, yy, c, g], az_s.at[slot, j], az_r.at[zz, yy], at(to, y, c)
        )

    def z_own(src, j, act_on):
        pl.when(z < A - 1)(lambda: act_on(z_gather(src, z, j, 0, z + 1)))
        pl.when(z > 0)(lambda: act_on(z_gather(src, z, j, 1, z - 1)))

    def z_onward(i, j, act_on):
        zz = partner(i)
        got = weights.at[:, zz, column(j), c, g]
        pl.when(inner)(lambda: act_on(z_gather(got, zz, j, 1 + i, onward[i])))

    def start(one):
        one.start()

    def x_gather(zz, yy):
        block = weights.at[:, zz, yy, c, g]
        return copy(block, block, ax_s.at[zz, yy], ax_r.at[zz, yy], x_peer)

    def core_gather(zz, yy, src):
        return copy(src, weights.at[:, zz, yy, c], ac_s.at[zz, yy], ac_r.at[zz, yy], core_peer)

    def go(one):
        one.start()
        pending.append(one)

    y_gather = copy(kern.at[:, g], weights.at[:, z, y, c, g], ay_s, ay_r, y_peer)
    go(y_gather)
    z_own(kern.at[:, g], 0, start)
    go(core_gather(z, y, kern))

    tile = pairs32.shape[1]

    def gelu_tile(i, carry):
        at_row = pl.multiple_of(i * tile, tile)
        v = act[pl.ds(at_row, tile), :].astype(F32)
        e = 0.5 * (1.0 + lax.erf(v * 0.7071067811865476))
        gelu = (v * e).astype(BF16).astype(F32)
        slope[pl.ds(at_row, tile), :] = e + v * jnp.exp(-0.5 * v * v) * 0.3989422804014327
        half = pl.multiple_of(i * (tile // 2), tile // 2)
        for j in range(cin // 128):
            lanes = slice(j * 128, j * 128 + 128)
            pairs32[j] = gelu[:, lanes]
            g2x[pl.ds(PAD + half, tile // 2), lanes] = (
                pairs32[j, pl.ds(0, tile // 2, stride=2), :]
                + pairs32[j, pl.ds(1, tile // 2, stride=2), :]
            )
        return carry

    lax.fori_loop(0, 2 * T2 // tile, gelu_tile, 0)
    gedge[0] = g2x[pl.ds(PAD, 16), :].astype(BF16)
    gedge[1] = g2x[pl.ds(PAD + T2 - 16, 16), :].astype(BF16)
    gl = copy(gedge.at[0], ghalo.at[1], gh_s.at[0], gh_r.at[1], left)
    gr = copy(gedge.at[1], ghalo.at[0], gh_s.at[1], gh_r.at[0], right)
    gl.start()
    gr.start()


    def take_z(i, j):
        zz, yy = partner(i), column(j)
        got = weights.at[:, zz, yy, c, g]
        copy(got, got, az_s.at[1 + i, j], az_r.at[zz, yy], y_peer).wait_recv()
        z_onward(i, j, start)
        go(x_gather(zz, yy))

    def take_x(i, yy):
        zz = partner(i)
        got = weights.at[:, zz, yy, c, 1 - g]
        copy(got, got, ax_s.at[zz, yy], ax_r.at[zz, yy], x_peer).wait_recv()
        go(core_gather(zz, yy, weights.at[:, zz, yy, c]))

    def take_core(i, yy):
        zz = partner(i)
        got = weights.at[:, zz, yy, 1 - c]
        copy(got, got, ac_s.at[zz, yy], ac_r.at[zz, yy], core_peer).wait_recv()

    def tap_dot(k):
        ds[k] = dx[pl.ds(PAD - step * (k - mid), T2), :].astype(BF16)
        half_z = A // 2
        for i in range(2):
            m = cin // 2
            term = jnp.dot(g2t[pl.ds(i * m, m), :], ds[k], preferred_element_type=F32)
            term = term.reshape(half_z, 2, 2, rows, cout)
            part[k, pl.ds(i * half_z, half_z)] = term
            send1[k, pl.ds(i * half_z, half_z)] = term.astype(BF16)
        go(copy(send1.at[k, :, :, 1 - c], recv1.at[k], r1_s.at[k], r1_r.at[k], core_peer))

    def tap_core(k):
        copy(send1.at[k, :, :, c], recv1.at[k], r1_s.at[k], r1_r.at[k], core_peer).wait_recv()
        for zz in range(A):
            send2[k, zz] = (part[k, zz, 1 - y, c] + recv1[k, zz, 1 - y].astype(F32)).astype(BF16)
        go(copy(send2.at[k], recv2.at[k], r2_s.at[k], r2_r.at[k], y_peer))
        for zz in range(A):
            part2[k, zz] = part[k, zz, y, c] + recv1[k, zz, y].astype(F32)

    def tap_y(k):
        copy(send2.at[k], recv2.at[k], r2_s.at[k], r2_r.at[k], y_peer).wait_recv()
        for zz in range(A):
            total = part2[k, zz] + recv2[k, zz].astype(F32)
            part2[k, zz] = total
            send3[k, zz] = total.astype(BF16)
        for i in range(1, A):
            zz = partner(i)
            go(copy(send3.at[k, zz], recv3.at[k, z], r3_s.at[k, i], r3_r.at[k, z], at(zz, y, c)))

    def tap_z(k):
        total = part2[k, z]
        for i in range(1, A):
            zz = partner(i)
            copy(
                send3.at[k, zz], recv3.at[k, zz], r3_s.at[k, i], r3_r.at[k, zz], at(zz, y, c)
            ).wait_recv()
            total = total + recv3[k, zz].astype(F32)
        kout[k] = total
        done = pltpu.make_async_copy(kout.at[k], kgrad.at[k], out_sem.at[k])
        done.start()
        leaving.append(done)

    own.wait()
    y_gather.wait_recv()
    across = weights.at[:, z, 1 - y, c, g]
    z_own(across, 1, start)
    go(x_gather(z, 1 - y))
    take_z(1, 0)
    cols = 128
    for i in range(cin // cols):
        g2t[pl.ds(i * cols, cols), :] = g2x[pl.ds(PAD, T2), pl.ds(i * cols, cols)].T.astype(BF16)

    keep_left = (p > 0).astype(F32)
    keep_right = (p < n - 1).astype(F32)
    for i in range(T2 // 128):
        dx[pl.ds(PAD + i * 128, 128), :] = 0.5 * cot[pl.ds(i * 128, 128), :].astype(F32)
    dl.wait_recv()
    dr.wait_recv()
    dx[pl.ds(0, PAD), :] = dhalo[0].astype(F32)[16 - PAD :] * (0.5 * keep_left)
    dx[pl.ds(PAD + T2, PAD), :] = dhalo[1].astype(F32)[:PAD] * (0.5 * keep_right)


    arrivals = ((1, 1), (2, 0), (2, 1), (3, 0))
    for k in range(taps):
        tap_dot(k)
        if k:
            tap_core(k - 1)
        if 0 < k < len(arrivals):
            take_z(*arrivals[k - 1])
    tap_core(taps - 1)
    take_z(3, 0)
    take_z(3, 1)
    gl.wait_recv()
    gr.wait_recv()
    g2x[pl.ds(0, PAD), :] = ghalo[0].astype(F32)[16 - PAD :] * keep_left
    g2x[pl.ds(PAD + T2, PAD), :] = ghalo[1].astype(F32)[:PAD] * keep_right
    take_x(0, 1 - y)
    take_x(1, y)
    take_x(1, 1 - y)
    tap_y(0)
    take_x(2, y)
    take_x(2, 1 - y)
    tap_y(1)
    take_x(3, y)
    take_x(3, 1 - y)
    for k in range(2, taps - 1):
        tap_y(k)
    for i in range(A):
        take_core(i, y)
        take_core(i, 1 - y)

    m = spread.shape[1] // 2

    def conv_tile(i, carry):
        base = pl.multiple_of(i * m, m)
        total = jnp.zeros((m, cout), F32)
        grad = jnp.zeros((m, cin), F32)
        window = g2x[pl.ds(base, m + 2 * PAD), :]
        for k in range(taps):
            off = PAD + step * (k - mid)
            w = weights[k].reshape(cin, cout)
            total += jnp.dot(
                window[off : off + m].astype(BF16), w, preferred_element_type=F32
            )
            grad += lax.dot_general(
                ds[k, pl.ds(base, m), :], w, (((1,), (1,)), ((), ())), preferred_element_type=F32
            )
        pooled[pl.ds(base, m), :] = (0.5 * total).astype(BF16)
        for j in range(cin // 128):
            lanes = slice(j * 128, j * 128 + 128)
            spread[j, pl.ds(0, m, stride=2), :] = grad[:, lanes]
            spread[j, pl.ds(1, m, stride=2), :] = grad[:, lanes]
            at_row = pl.multiple_of(i * 2 * m, 2 * m)
            igrad[pl.ds(at_row, 2 * m), lanes] = (
                spread[j] * slope[pl.ds(at_row, 2 * m), lanes]
            ).astype(BF16)
        return carry

    lax.fori_loop(0, 1, conv_tile, 0)
    tap_y(taps - 1)
    lax.fori_loop(1, T2 // m, conv_tile, 0)

    for k in range(taps):
        tap_z(k)

    for one in leaving:
        one.wait()
    for one in (dl, dr, gl, gr):
        one.wait_send()
    for one in pending:
        one.wait_send()
    z_own(kern.at[:, g], 0, lambda one: one.wait_send())
    z_own(across, 1, lambda one: one.wait_send())
    for i in range(1, A):
        for j in range(2):
            z_onward(i, j, lambda one: one.wait_send())


def on_device_fused(activations, kernel, cotangent):
    n = lax.axis_size("pos")
    A = n // 4
    rows, taps, cout = kernel.shape
    T2 = cotangent.shape[0]
    cin = activations.shape[1]
    dims = (n, A, taps, rows, T2, cin, cout)
    kern = jnp.transpose(kernel, (1, 0, 2)).reshape(taps, 2, rows // 2, cout)
    vmem = pl.BlockSpec(memory_space=pltpu.VMEM)
    DMA = pltpu.SemaphoreType.DMA
    pooled, igrad, kgrad = pl.pallas_call(
        functools.partial(step_kernel, dims),
        out_shape=(
            jax.ShapeDtypeStruct((T2, cout), BF16),
            jax.ShapeDtypeStruct((2 * T2, cin), BF16),
            jax.ShapeDtypeStruct((taps, rows, cout), F32),
        ),
        in_specs=[vmem, pl.BlockSpec(memory_space=pltpu.HBM), vmem],
        out_specs=(vmem, vmem, pl.BlockSpec(memory_space=pltpu.HBM)),
        scratch_shapes=[
            pltpu.VMEM((taps, A, 2, 2, 2, rows // 2, cout), BF16),
            pltpu.VMEM((2 * T2, cin), F32),
            pltpu.VMEM((cin // 128, 128, 128), F32),
            pltpu.VMEM((T2 + 2 * PAD, cin), F32),
            pltpu.VMEM((cin, T2), BF16),
            pltpu.VMEM((T2 + 2 * PAD, cout), F32),
            pltpu.VMEM((taps, T2, cout), BF16),
            pltpu.VMEM((taps, A, 2, 2, rows, cout), F32),
            pltpu.VMEM((taps, A, 2, 2, rows, cout), BF16),
            pltpu.VMEM((taps, A, 2, rows, cout), BF16),
            pltpu.VMEM((taps, A, rows, cout), F32),
            pltpu.VMEM((taps, A, rows, cout), BF16),
            pltpu.VMEM((taps, A, rows, cout), BF16),
            pltpu.VMEM((taps, A, rows, cout), BF16),
            pltpu.VMEM((taps, A, rows, cout), BF16),
            pltpu.VMEM((2, 16, cin), BF16),
            pltpu.VMEM((2, 16, cin), BF16),
            pltpu.VMEM((2, 16, cout), BF16),
            pltpu.VMEM((cin // 128, 512, 128), F32),
            pltpu.VMEM((taps, rows, cout), F32),
            DMA, DMA((taps,)), DMA((2,)), DMA((2,)), DMA((2,)), DMA((2,)),
            DMA((A + 1, 2)), DMA((A, 2)), DMA, DMA,
            DMA((A, 2)), DMA((A, 2)), DMA((A, 2)), DMA((A, 2)),
            DMA((taps,)), DMA((taps,)), DMA((taps,)), DMA((taps,)),
            DMA((taps, A)), DMA((taps, A)),
        ],
        compiler_params=pltpu.CompilerParams(
            collective_id=0, has_side_effects=True, vmem_limit_bytes=50 << 20
        ),
    )(activations, kern, cotangent)
    return pooled, igrad, jnp.transpose(kgrad, (1, 0, 2))


def solution(mesh):
    placed = (P(("groups", "pos"), None), P("pos", None, None), P(("groups", "pos"), None))
    n = mesh.shape["pos"]
    fused = n == 16 and mesh.shape["groups"] == 2
    return jax.shard_map(
        on_device_fused if fused else on_device,
        mesh=mesh,
        in_specs=placed,
        out_specs=(
            P(("groups", "pos"), None),
            P(("groups", "pos"), None),
            P(("groups", "pos"), None, None),
        ),
        check_vma=False,
    )
```
